32 devices in a mesh: blk: 8 (over z, x), rows: 4 (over y, core).
Axes of the slice: x: 2, y: 2, z: 4, core: 2. Of those that a mesh axis runs over, the one named last changes fastest.
Arguments:
- patterns: bfloat16 [2048, 4096], P('blk', 'rows'), may hold values from -6 to 6
- dictionary: bfloat16 [16384, 4096], P('blk', 'rows'), may hold values from -6 to 6
- codes: bfloat16 [2048, 256], P('blk'), may hold values from -6 to 6
- support: int32 [2048, 4], P('blk'), may hold values from 0 to 7, all different within a row
- wanted: int32 [8, 8], P('blk'), may hold values from 0 to 31
Outputs:
- dictionary_out: bfloat16 [16384, 4096], P('blk', 'rows')
- codes_out: float32 [2048, 256], P('blk')
The draws below stay inside these ranges and needn't reach their ends.
Inputs may be any that keep to these rules, and one draw needn't show every extreme that they name: `support`: the 4 entries of a row are different, and every slot is named by some pattern.
All inputs are finite; a program needn't handle non-finite values.
Results may differ from the reference program's by a relative error of at most 0.014.
Values may be sent and summed in bfloat16 or wider, within the bound.
A program may use at most 64 MiB of HBM per device.

```python
import jax
import jax.numpy as jnp
from jax import lax

PIXELS = 4096
BLOCK = 64
ABLK_DEV = 32
SUPP = 4
P_DEV = 256
REGIONS = 8
PATTERNS = 2048
ATOMS = 16384
N_BLK = 8


def plant(array, rng, low, high):
    index_at = [jax.random.randint(jax.random.fold_in(rng, axis), (), 0, length) for axis, length in enumerate(array.shape)]
    main_axis = array.shape.index(max(array.shape))
    neighbour = index_at[:main_axis] + [(index_at[main_axis] + 1) % array.shape[main_axis]] + index_at[main_axis + 1:]
    return array.at[tuple(index_at)].set(low).at[tuple(neighbour)].set(high)


def shard_levels(key, extent, pieces, low, high):
    level = 1.0
    for axis_at, parts in pieces:
        draws = jax.random.uniform(jax.random.fold_in(jax.random.fold_in(key, 6), axis_at), (parts,), jnp.float32, low / len(pieces), high / len(pieces))
        level = level * jnp.repeat(jnp.exp(draws), extent[axis_at] // parts).reshape((-1,) + (1,) * (len(extent) - 1 - axis_at))
    return level


def different_ones(stream_key, rows, amount, top, lift):
    sequence = jax.random.permutation(jax.random.fold_in(stream_key, 1), amount)
    pull = sequence
    for power in range(3):
        pull = pull * pull // amount
    pull = pull * lift // amount
    chance = jax.random.randint(jax.random.fold_in(stream_key, 2), (rows, amount), 0, 4096) + pull
    fixed_rows = jax.random.permutation(jax.random.fold_in(stream_key, 3), rows)[jnp.arange(amount) % rows]
    chance = jnp.where(jnp.arange(rows)[:, None] == fixed_rows[None, :], 1 << 14, chance)
    score = chance * amount + jnp.arange(amount)
    return lax.top_k(score.astype(jnp.int32), top)[1].astype(jnp.int32)


def normal_values(stream_key, dims, width, reach, shards=(), kind=jnp.bfloat16):
    result = width * jax.random.normal(stream_key, dims, jnp.float32)
    if shards:
        result = result * shard_levels(stream_key, dims, shards, -0.22, 0.18)
    return jnp.clip(result, -reach, reach).astype(kind)


def setup_inputs(seed: int = 0) -> dict:
    splits = jax.random.split(jax.random.key(seed), 6)
    return {
        "patterns": normal_values(splits[0], (PATTERNS, PIXELS), 1.0, 6.0, ((0, 8), (1, 4))),
        "dictionary": normal_values(splits[1], (ATOMS, PIXELS), 1.0, 6.0, ((0, 8), (1, 4))),
        "codes": normal_values(splits[2], (PATTERNS, SUPP * BLOCK), 1.0, 6.0, ((0, 8),)),
        "support": different_ones(splits[3], PATTERNS, N_BLK, SUPP, 8192),
        "wanted": plant(jax.random.randint(splits[4], (REGIONS, N_BLK), 0, ABLK_DEV), jax.random.fold_in(splits[4], 1), 0, ABLK_DEV - 1).astype(jnp.int32),
    }


CODE_RATE = 0.05
ATOM_RATE = 0.2


def reference(patterns, dictionary, codes, support, wanted):
    scale_factor = (SUPP * BLOCK) ** -0.5
    total_blocks = ABLK_DEV * N_BLK
    slot_ids = jnp.arange(N_BLK, dtype=jnp.int32)
    block_ids = (slot_ids[None, :] * ABLK_DEV + wanted).astype(jnp.int32)
    pattern_regions = patterns.reshape(N_BLK, P_DEV, PIXELS)
    support_regions = support.reshape(N_BLK, P_DEV, SUPP)
    atoms_now = dictionary
    codes_now = codes
    for step_index in range(2):
        blocks_now = atoms_now.reshape(total_blocks, BLOCK, PIXELS)
        code_regions = codes_now.astype(jnp.bfloat16).reshape(N_BLK, P_DEV, SUPP, BLOCK)

        def region_work(carry, items):
            region_rows, region_codes, region_support, region_blocks = items
            panels = jnp.take(blocks_now, region_blocks, axis=0).reshape(N_BLK * BLOCK, PIXELS)
            picker = (region_support[:, :, None] == slot_ids[None, None, :]).astype(jnp.float32)
            dense = jnp.einsum("psn,pse->pne", picker, region_codes.astype(jnp.float32),
                               precision=lax.Precision.HIGHEST)
            dense = dense.astype(jnp.bfloat16).reshape(P_DEV, N_BLK * BLOCK)
            rebuilt = scale_factor * jnp.dot(dense, panels, preferred_element_type=jnp.float32)
            residual = (region_rows.astype(jnp.float32) - rebuilt).astype(jnp.bfloat16)
            correlated = jnp.dot(residual, panels.T, preferred_element_type=jnp.float32)
            code_grad = scale_factor * jnp.einsum("psn,pne->pse", picker,
                                                  correlated.reshape(P_DEV, N_BLK, BLOCK),
                                                  precision=lax.Precision.HIGHEST)
            atom_terms = scale_factor * jnp.dot(dense.T, residual, preferred_element_type=jnp.float32)
            carry = carry.at[region_blocks].add(atom_terms.reshape(N_BLK, BLOCK, PIXELS))
            return carry, code_grad

        grad_start = jnp.zeros((total_blocks, BLOCK, PIXELS), jnp.float32)
        atom_grad, code_grads = lax.scan(region_work, grad_start,
                                         (pattern_regions, code_regions, support_regions, block_ids))
        atoms_now = (atoms_now.astype(jnp.float32)
                     + ATOM_RATE * atom_grad.reshape(ATOMS, PIXELS)).astype(jnp.bfloat16)
        codes_now = codes_now.astype(jnp.float32) + CODE_RATE * code_grads.reshape(PATTERNS, SUPP * BLOCK)
    return atoms_now, codes_now
```

```python
import functools

import jax
import jax.numpy as jnp
from jax import lax
from jax.experimental import pallas as pl
from jax.experimental.pallas import tpu as pltpu
from jax.sharding import PartitionSpec as P

CODE_RATE = 0.05
ATOM_RATE = 0.2
CHUNK = 256
MESH = pl.DeviceIdType.MESH


def steps_kernel(
    owners, row_count, block_width, chunk, scale_factor,
    same_ref, support_ref, codes_ref, patterns_ref, slots_ref,
    slots_out, codes_out,
    panels, arrived, terms, slots_next, dense, correlated, code_parts,
    send_sems, recv_sems, code_send, code_recv,
):
    me = lax.axis_index("blk")
    my_row = lax.axis_index("rows")
    pattern_rows, pixel_count = patterns_ref.shape
    chunks = pixel_count // chunk
    support_count = support_ref.shape[1]
    lanes = 128
    per_lane = lanes // block_width

    barrier = pltpu.get_barrier_semaphore()
    for j in range(1, owners):
        pl.semaphore_signal(
            barrier, inc=1, device_id={"blk": lax.rem(me + j, owners)}, device_id_type=MESH
        )
    for j in range(1, row_count):
        pl.semaphore_signal(
            barrier, inc=1, device_id={"rows": lax.rem(my_row + j, row_count)}, device_id_type=MESH
        )
    pl.semaphore_wait(barrier, owners + row_count - 2)

    def columns(k):
        return pl.ds(pl.multiple_of(k * chunk, chunk), chunk)

    def block_copy(phase, k, j, source, target):
        return pltpu.make_async_remote_copy(
            src_ref=source,
            dst_ref=target,
            send_sem=send_sems.at[phase, k, j],
            recv_sem=recv_sems.at[phase, k, j],
            device_id={"blk": lax.rem(me + j, owners)},
            device_id_type=MESH,
        )

    def wait_arrivals(phase, k, target):
        for j in range(1, owners):
            block_copy(phase, k, j, target, target).wait_recv()

    def send_panels(k, _):
        for j in range(1, owners):
            block_copy(
                0, k, j,
                slots_ref.at[lax.rem(me + j, owners), :, columns(k)],
                panels.at[0, k, me],
            ).start()
        panels[0, k, me] = slots_ref[me, :, columns(k)]
        return 0

    lax.fori_loop(0, chunks, send_panels, 0)

    half = lax.broadcasted_iota(jnp.int32, (pattern_rows, lanes), 1) // block_width

    def matches(s, m):
        return support_ref[:, s:s + 1] == half + m * per_lane

    def spread(codes_now):
        pieces = []
        for s in range(support_count):
            piece = codes_now[:, s * block_width:(s + 1) * block_width]
            pieces.append(jnp.concatenate([piece] * per_lane, axis=1))
        for m in range(owners // per_lane):
            total = jnp.zeros((pattern_rows, lanes), jnp.float32)
            for s in range(support_count):
                total = jnp.where(matches(s, m), pieces[s], total)
            dense[:, m * lanes:(m + 1) * lanes] = total.astype(jnp.bfloat16)

    def pick():
        pieces = []
        for s in range(support_count):
            total = jnp.zeros((pattern_rows, lanes), jnp.float32)
            for m in range(owners // per_lane):
                total = jnp.where(matches(s, m), correlated[:, m * lanes:(m + 1) * lanes], total)
            folded = total[:, :block_width]
            for h in range(1, per_lane):
                folded = folded + total[:, h * block_width:(h + 1) * block_width]
            pieces.append(folded)
        return scale_factor * jnp.concatenate(pieces, axis=1)

    def code_copy(step, j):
        return pltpu.make_async_remote_copy(
            src_ref=code_parts.at[step, my_row],
            dst_ref=code_parts.at[step, my_row],
            send_sem=code_send.at[step, j],
            recv_sem=code_recv.at[step, j],
            device_id={"rows": lax.rem(my_row + j, row_count)},
            device_id_type=MESH,
        )

    codes_out[...] = codes_ref[...].astype(jnp.float32)

    for step in range(2):
        spread(codes_out[...].astype(jnp.bfloat16).astype(jnp.float32))
        correlated[...] = jnp.zeros_like(correlated)

        def region_chunk(k, _, step=step):
            wait_arrivals(2 * step, k, panels.at[step, k, 0])
            panel = panels[step, k].reshape(owners * block_width, chunk)
            coefficients = dense[...]
            rebuilt = scale_factor * jnp.dot(
                coefficients, panel, preferred_element_type=jnp.float32
            )
            residual = (patterns_ref[:, columns(k)].astype(jnp.float32) - rebuilt).astype(
                jnp.bfloat16
            )
            atom_terms = scale_factor * lax.dot_general(
                coefficients, residual, (((0,), (0,)), ((), ())),
                preferred_element_type=jnp.float32,
            )
            terms[step, k] = atom_terms.astype(jnp.bfloat16).reshape(owners, block_width, chunk)
            for j in range(1, owners):
                block_copy(
                    2 * step + 1, k, j,
                    terms.at[step, k, lax.rem(me + j, owners)],
                    arrived.at[step, k, me],
                ).start()
            arrived[step, k, me] = terms[step, k, me]
            correlated[...] += lax.dot_general(
                residual, panel, (((1,), (1,)), ((), ())), preferred_element_type=jnp.float32
            )
            return 0

        lax.fori_loop(0, chunks, region_chunk, 0)
        code_parts[step, my_row] = pick().astype(jnp.bfloat16)
        for j in range(1, row_count):
            code_copy(step, j).start()

        def owner_chunk(k, _, step=step):
            wait_arrivals(2 * step + 1, k, arrived.at[step, k, 0])

            def one_slot(r, _):
                total = jnp.zeros((block_width, chunk), jnp.float32)
                for q in range(owners):
                    total = total + same_ref[r, q] * arrived[step, k, q].astype(jnp.float32)
                before = slots_ref[r, :, columns(k)] if step == 0 else slots_next[k, r]
                after = (before.astype(jnp.float32) + ATOM_RATE * total).astype(jnp.bfloat16)
                if step == 0:
                    slots_next[k, r] = after
                else:
                    slots_out[r, :, columns(k)] = after
                return 0

            lax.fori_loop(0, owners, one_slot, 0)
            if step == 0:
                for j in range(1, owners):
                    block_copy(
                        2, k, j,
                        slots_next.at[k, lax.rem(me + j, owners)],
                        panels.at[1, k, me],
                    ).start()
                panels[1, k, me] = slots_next[k, me]
            return 0

        lax.fori_loop(0, chunks, owner_chunk, 0)
        for j in range(1, row_count):
            code_copy(step, j).wait_recv()
        total = code_parts[step, 0].astype(jnp.float32)
        for i in range(1, row_count):
            total = total + code_parts[step, i].astype(jnp.float32)
        codes_out[...] += CODE_RATE * total

    def drain(k, _):
        for phase in range(4):
            for j in range(1, owners):
                block_copy(phase, k, j, terms.at[0, k, 0], terms.at[0, k, 0]).wait_send()
        return 0

    lax.fori_loop(0, chunks, drain, 0)
    for step in range(2):
        for j in range(1, row_count):
            code_copy(step, j).wait_send()


def put_kernel(group, selected_ref, dictionary_ref, slots_ref, out_ref):
    first = pl.program_id(0) * group
    for i in range(group):
        chosen = selected_ref[first + i]

        @pl.when(chosen >= 0)
        def _():
            out_ref[i] = slots_ref[jnp.maximum(chosen, 0)]

        @pl.when(chosen < 0)
        def _():
            out_ref[i] = dictionary_ref[i]


def local(patterns, dictionary, codes, support, wanted):
    owners = lax.axis_size("blk")
    row_count = lax.axis_size("rows")
    pattern_rows, pixel_count = patterns.shape
    support_count = support.shape[1]
    code_width = codes.shape[1]
    block_width = code_width // support_count
    owned_blocks = dictionary.shape[0] // block_width
    scale_factor = code_width ** (-0.5)
    chunk = min(CHUNK, pixel_count)
    chunks = pixel_count // chunk
    asked = lax.all_to_all(wanted, "blk", split_axis=1, concat_axis=0, tiled=True)[:, 0]
    same = (asked[:, None] == asked[None, :]).astype(jnp.float32)
    blocks = dictionary.reshape(owned_blocks, block_width, pixel_count)
    slots = jnp.take(blocks, asked, axis=0)
    vmem = pl.BlockSpec(memory_space=pltpu.VMEM)
    bf16 = jnp.bfloat16
    slots_after, codes_after = pl.pallas_call(
        functools.partial(steps_kernel, owners, row_count, block_width, chunk, scale_factor),
        out_shape=(
            jax.ShapeDtypeStruct((owners, block_width, pixel_count), bf16),
            jax.ShapeDtypeStruct((pattern_rows, code_width), jnp.float32),
        ),
        in_specs=[pl.BlockSpec(memory_space=pltpu.SMEM)] + [vmem] * 4,
        out_specs=(vmem, vmem),
        scratch_shapes=[
            pltpu.VMEM((2, chunks, owners, block_width, chunk), bf16),
            pltpu.VMEM((2, chunks, owners, block_width, chunk), bf16),
            pltpu.VMEM((2, chunks, owners, block_width, chunk), bf16),
            pltpu.VMEM((chunks, owners, block_width, chunk), bf16),
            pltpu.VMEM((pattern_rows, owners * block_width), bf16),
            pltpu.VMEM((pattern_rows, owners * block_width), jnp.float32),
            pltpu.VMEM((2, row_count, pattern_rows, code_width), bf16),
            pltpu.SemaphoreType.DMA((4, chunks, owners)),
            pltpu.SemaphoreType.DMA((4, chunks, owners)),
            pltpu.SemaphoreType.DMA((2, row_count)),
            pltpu.SemaphoreType.DMA((2, row_count)),
        ],
        compiler_params=pltpu.CompilerParams(
            collective_id=0, has_side_effects=True, vmem_limit_bytes=40 * 1024 * 1024
        ),
    )(same, support, codes, patterns, slots)
    slot_ids = jnp.arange(owners, dtype=jnp.int32)
    block_ids = jnp.arange(owned_blocks, dtype=jnp.int32)
    selected = jnp.max(
        jnp.where(asked[None, :] == block_ids[:, None], slot_ids[None, :], -1), axis=1
    )
    group = 4
    dictionary_after = pl.pallas_call(
        functools.partial(put_kernel, group),
        out_shape=jax.ShapeDtypeStruct(blocks.shape, bf16),
        grid_spec=pltpu.PrefetchScalarGridSpec(
            num_scalar_prefetch=1,
            grid=(owned_blocks // group,),
            in_specs=[
                pl.BlockSpec((group, block_width, pixel_count), lambda i, sel: (i, 0, 0)),
                pl.BlockSpec((owners, block_width, pixel_count), lambda i, sel: (0, 0, 0)),
            ],
            out_specs=pl.BlockSpec((group, block_width, pixel_count), lambda i, sel: (i, 0, 0)),
        ),
    )(selected, blocks, slots_after)
    return (dictionary_after.reshape(dictionary.shape), codes_after)


def solution(mesh):
    placed = (P("blk", "rows"), P("blk", "rows"), P("blk", None), P("blk", None), P("blk", None))
    return jax.shard_map(
        local,
        mesh=mesh,
        in_specs=placed,
        out_specs=(P("blk", "rows"), P("blk", None)),
        check_vma=False,
    )
```

```python
import functools

import jax
import jax.numpy as jnp
from jax import lax
from jax.experimental import pallas as pl
from jax.experimental.pallas import tpu as pltpu
from jax.sharding import PartitionSpec as P

CODE_RATE = 0.05
ATOM_RATE = 0.2
CHUNK = 256
MESH = pl.DeviceIdType.MESH


def steps_kernel(
    owners, row_count, block_width, chunk, scale_factor,
    wanted_ref, support_hbm, codes_hbm, patterns_hbm, dictionary_hbm,
    dictionary_out, codes_out,
    support_ref, codes_ref, patterns_ref, pool, asked_vmem, asked_smem, chosen,
    panels, arrived, terms, slots_before, slots_next, dense, correlated, code_parts,
    send_sems, recv_sems, code_send, code_recv, ask_send, ask_recv, load_sems,
):
    me = lax.axis_index("blk")
    my_row = lax.axis_index("rows")
    pattern_rows, pixel_count = patterns_ref.shape
    owned_blocks = dictionary_out.shape[0]
    chunks = pixel_count // chunk
    loads = (
        pltpu.make_async_copy(
            dictionary_hbm, pool.at[pl.ds(0, owned_blocks)], load_sems.at[0]
        ),
        pltpu.make_async_copy(codes_hbm, codes_ref, load_sems.at[1]),
        pltpu.make_async_copy(support_hbm, support_ref, load_sems.at[2]),
        pltpu.make_async_copy(patterns_hbm, patterns_ref, load_sems.at[3]),
    )
    for load in loads:
        load.start()
    support_count = support_ref.shape[1]
    lanes = 128
    per_lane = lanes // block_width

    barrier = pltpu.get_barrier_semaphore()
    for j in range(1, owners):
        pl.semaphore_signal(
            barrier, inc=1, device_id={"blk": lax.rem(me + j, owners)}, device_id_type=MESH
        )
    for j in range(1, row_count):
        pl.semaphore_signal(
            barrier, inc=1, device_id={"rows": lax.rem(my_row + j, row_count)}, device_id_type=MESH
        )
    pl.semaphore_wait(barrier, owners + row_count - 2)

    def columns(k):
        return pl.ds(pl.multiple_of(k * chunk, chunk), chunk)

    def block_copy(phase, k, j, source, target):
        return pltpu.make_async_remote_copy(
            src_ref=source,
            dst_ref=target,
            send_sem=send_sems.at[phase, k, j],
            recv_sem=recv_sems.at[phase, k, j],
            device_id={"blk": lax.rem(me + j, owners)},
            device_id_type=MESH,
        )

    def wait_arrivals(phase, k, target):
        for j in range(1, owners):
            block_copy(phase, k, j, target, target).wait_recv()

    def ask_copy(j):
        return pltpu.make_async_remote_copy(
            src_ref=wanted_ref,
            dst_ref=asked_vmem.at[me],
            send_sem=ask_send.at[j],
            recv_sem=ask_recv.at[j],
            device_id={"blk": lax.rem(me + j, owners)},
            device_id_type=MESH,
        )

    for j in range(1, owners):
        ask_copy(j).start()
    asked_vmem[me] = wanted_ref[...]
    for j in range(1, owners):
        ask_copy(j).wait_recv()
    move = pltpu.make_async_copy(asked_vmem, asked_smem, load_sems.at[4])
    move.start()
    move.wait()
    loads[0].wait()

    def asked(r):
        return asked_smem[r, 0, me]

    def send_panels(k, _):
        def gather(r, _):
            slots_before[k, r] = pool[asked(r), :, columns(k)]
            return 0

        lax.fori_loop(0, owners, gather, 0)
        for j in range(1, owners):
            block_copy(
                0, k, j, slots_before.at[k, lax.rem(me + j, owners)], panels.at[0, k, me]
            ).start()
        panels[0, k, me] = slots_before[k, me]
        return 0

    lax.fori_loop(0, chunks, send_panels, 0)

    def choose(b, _):
        place = b
        for r in range(owners):
            place = jnp.where(asked(r) == b, owned_blocks + r, place)
        chosen[b] = place
        return 0

    lax.fori_loop(0, owned_blocks, choose, 0)
    for load in loads[1:]:
        load.wait()

    half = lax.broadcasted_iota(jnp.int32, (pattern_rows, lanes), 1) // block_width

    def matches(s, m):
        return support_ref[:, s:s + 1] == half + m * per_lane

    def spread(codes_now):
        pieces = []
        for s in range(support_count):
            piece = codes_now[:, s * block_width:(s + 1) * block_width]
            pieces.append(jnp.concatenate([piece] * per_lane, axis=1))
        for m in range(owners // per_lane):
            total = jnp.zeros((pattern_rows, lanes), jnp.float32)
            for s in range(support_count):
                total = jnp.where(matches(s, m), pieces[s], total)
            dense[:, m * lanes:(m + 1) * lanes] = total.astype(jnp.bfloat16)

    def pick():
        pieces = []
        for s in range(support_count):
            total = jnp.zeros((pattern_rows, lanes), jnp.float32)
            for m in range(owners // per_lane):
                total = jnp.where(matches(s, m), correlated[:, m * lanes:(m + 1) * lanes], total)
            folded = total[:, :block_width]
            for h in range(1, per_lane):
                folded = folded + total[:, h * block_width:(h + 1) * block_width]
            pieces.append(folded)
        return scale_factor * jnp.concatenate(pieces, axis=1)

    def code_copy(step, j):
        return pltpu.make_async_remote_copy(
            src_ref=code_parts.at[step, my_row],
            dst_ref=code_parts.at[step, my_row],
            send_sem=code_send.at[step, j],
            recv_sem=code_recv.at[step, j],
            device_id={"rows": lax.rem(my_row + j, row_count)},
            device_id_type=MESH,
        )

    codes_out[...] = codes_ref[...].astype(jnp.float32)

    for step in range(2):
        spread(codes_out[...].astype(jnp.bfloat16).astype(jnp.float32))
        correlated[...] = jnp.zeros_like(correlated)

        def region_chunk(k, _, step=step):
            wait_arrivals(2 * step, k, panels.at[step, k, 0])
            panel = panels[step, k].reshape(owners * block_width, chunk)
            coefficients = dense[...]
            rebuilt = scale_factor * jnp.dot(
                coefficients, panel, preferred_element_type=jnp.float32
            )
            residual = (patterns_ref[:, columns(k)].astype(jnp.float32) - rebuilt).astype(
                jnp.bfloat16
            )
            atom_terms = scale_factor * lax.dot_general(
                coefficients, residual, (((0,), (0,)), ((), ())),
                preferred_element_type=jnp.float32,
            )
            terms[step, k] = atom_terms.astype(jnp.bfloat16).reshape(owners, block_width, chunk)
            for j in range(1, owners):
                block_copy(
                    2 * step + 1, k, j,
                    terms.at[step, k, lax.rem(me + j, owners)],
                    arrived.at[step, k, me],
                ).start()
            arrived[step, k, me] = terms[step, k, me]
            correlated[...] += lax.dot_general(
                residual, panel, (((1,), (1,)), ((), ())), preferred_element_type=jnp.float32
            )
            return 0

        lax.fori_loop(0, chunks, region_chunk, 0)
        code_parts[step, my_row] = pick().astype(jnp.bfloat16)
        for j in range(1, row_count):
            code_copy(step, j).start()

        def owner_chunk(k, _, step=step):
            wait_arrivals(2 * step + 1, k, arrived.at[step, k, 0])

            def one_slot(r, _):
                total = jnp.zeros((block_width, chunk), jnp.float32)
                for q in range(owners):
                    same = jnp.where(asked(r) == asked(q), 1.0, 0.0).astype(jnp.float32)
                    total = total + same * arrived[step, k, q].astype(jnp.float32)
                before = slots_before[k, r] if step == 0 else slots_next[k, r]
                after = (before.astype(jnp.float32) + ATOM_RATE * total).astype(jnp.bfloat16)
                if step == 0:
                    slots_next[k, r] = after
                else:
                    pool[owned_blocks + r, :, columns(k)] = after
                return 0

            lax.fori_loop(0, owners, one_slot, 0)
            if step == 0:
                for j in range(1, owners):
                    block_copy(
                        2, k, j,
                        slots_next.at[k, lax.rem(me + j, owners)],
                        panels.at[1, k, me],
                    ).start()
                panels[1, k, me] = slots_next[k, me]
            return 0

        lax.fori_loop(0, chunks, owner_chunk, 0)
        for j in range(1, row_count):
            code_copy(step, j).wait_recv()
        total = code_parts[step, 0].astype(jnp.float32)
        for i in range(1, row_count):
            total = total + code_parts[step, i].astype(jnp.float32)
        codes_out[...] += CODE_RATE * total

    def place_block(b, _):
        dictionary_out[b] = pool[chosen[b]]
        return 0

    lax.fori_loop(0, owned_blocks, place_block, 0)

    def drain(k, _):
        for phase in range(4):
            for j in range(1, owners):
                block_copy(phase, k, j, terms.at[0, k, 0], terms.at[0, k, 0]).wait_send()
        return 0

    lax.fori_loop(0, chunks, drain, 0)
    for step in range(2):
        for j in range(1, row_count):
            code_copy(step, j).wait_send()
    for j in range(1, owners):
        ask_copy(j).wait_send()


def local(patterns, dictionary, codes, support, wanted):
    owners = lax.axis_size("blk")
    row_count = lax.axis_size("rows")
    pattern_rows, pixel_count = patterns.shape
    support_count = support.shape[1]
    code_width = codes.shape[1]
    block_width = code_width // support_count
    owned_blocks = dictionary.shape[0] // block_width
    scale_factor = code_width ** (-0.5)
    chunk = min(CHUNK, pixel_count)
    chunks = pixel_count // chunk
    blocks = dictionary.reshape(owned_blocks, block_width, pixel_count)
    vmem = pl.BlockSpec(memory_space=pltpu.VMEM)
    bf16 = jnp.bfloat16
    hbm = pl.BlockSpec(memory_space=pl.ANY)
    dictionary_after, codes_after = pl.pallas_call(
        functools.partial(steps_kernel, owners, row_count, block_width, chunk, scale_factor),
        out_shape=(
            jax.ShapeDtypeStruct((owned_blocks, block_width, pixel_count), bf16),
            jax.ShapeDtypeStruct((pattern_rows, code_width), jnp.float32),
        ),
        in_specs=[vmem] + [hbm] * 4,
        out_specs=(vmem, vmem),
        scratch_shapes=[
            pltpu.VMEM(support.shape, jnp.int32),
            pltpu.VMEM(codes.shape, bf16),
            pltpu.VMEM(patterns.shape, bf16),
            pltpu.VMEM((owned_blocks + owners, block_width, pixel_count), bf16),
            pltpu.VMEM((owners,) + wanted.shape, jnp.int32),
            pltpu.SMEM((owners,) + wanted.shape, jnp.int32),
            pltpu.SMEM((owned_blocks,), jnp.int32),
            pltpu.VMEM((2, chunks, owners, block_width, chunk), bf16),
            pltpu.VMEM((2, chunks, owners, block_width, chunk), bf16),
            pltpu.VMEM((2, chunks, owners, block_width, chunk), bf16),
            pltpu.VMEM((chunks, owners, block_width, chunk), bf16),
            pltpu.VMEM((chunks, owners, block_width, chunk), bf16),
            pltpu.VMEM((pattern_rows, owners * block_width), bf16),
            pltpu.VMEM((pattern_rows, owners * block_width), jnp.float32),
            pltpu.VMEM((2, row_count, pattern_rows, code_width), bf16),
            pltpu.SemaphoreType.DMA((4, chunks, owners)),
            pltpu.SemaphoreType.DMA((4, chunks, owners)),
            pltpu.SemaphoreType.DMA((2, row_count)),
            pltpu.SemaphoreType.DMA((2, row_count)),
            pltpu.SemaphoreType.DMA((owners,)),
            pltpu.SemaphoreType.DMA((owners,)),
            pltpu.SemaphoreType.DMA((5,)),
        ],
        compiler_params=pltpu.CompilerParams(
            collective_id=0, has_side_effects=True, vmem_limit_bytes=40 * 1024 * 1024
        ),
    )(wanted, support, codes, patterns, blocks)
    return (dictionary_after.reshape(dictionary.shape), codes_after)


def solution(mesh):
    placed = (P("blk", "rows"), P("blk", "rows"), P("blk", None), P("blk", None), P("blk", None))
    return jax.shard_map(
        local,
        mesh=mesh,
        in_specs=placed,
        out_specs=(P("blk", "rows"), P("blk", None)),
        check_vma=False,
    )
```

```python
import functools

import jax
import jax.numpy as jnp
from jax import lax
from jax.experimental import pallas as pl
from jax.experimental.pallas import tpu as pltpu
from jax.sharding import PartitionSpec as P

CODE_RATE = 0.05
ATOM_RATE = 0.2
CHUNK = 256
MESH = pl.DeviceIdType.MESH


def steps_kernel(
    owners, row_count, block_width, chunk, scale_factor,
    wanted_ref, support_hbm, codes_hbm, patterns_hbm, dictionary_hbm,
    dictionary_out, codes_out,
    support_ref, codes_ref, patterns_ref, pool, asked_vmem, asked_smem, chosen,
    panels, arrived, terms, slots_before, slots_next, dense, correlated, code_parts,
    send_sems, recv_sems, code_send, code_recv, ask_send, ask_recv, load_sems,
):
    me = lax.axis_index("blk")
    my_row = lax.axis_index("rows")
    pattern_rows, pixel_count = patterns_ref.shape
    owned_blocks = dictionary_out.shape[0]
    chunks = pixel_count // chunk
    loads = (
        pltpu.make_async_copy(
            dictionary_hbm, pool.at[pl.ds(0, owned_blocks)], load_sems.at[0]
        ),
        pltpu.make_async_copy(codes_hbm, codes_ref, load_sems.at[1]),
        pltpu.make_async_copy(support_hbm, support_ref, load_sems.at[2]),
        pltpu.make_async_copy(patterns_hbm, patterns_ref, load_sems.at[3]),
    )
    for load in loads:
        load.start()
    support_count = support_ref.shape[1]
    lanes = 128
    per_lane = lanes // block_width

    barrier = pltpu.get_barrier_semaphore()
    for j in range(1, owners):
        pl.semaphore_signal(
            barrier, inc=1, device_id={"blk": lax.rem(me + j, owners)}, device_id_type=MESH
        )
    for j in range(1, row_count):
        pl.semaphore_signal(
            barrier, inc=1, device_id={"rows": lax.rem(my_row + j, row_count)}, device_id_type=MESH
        )
    pl.semaphore_wait(barrier, owners + row_count - 2)

    def columns(k):
        return pl.ds(pl.multiple_of(k * chunk, chunk), chunk)

    def block_copy(phase, k, j, source, target):
        return pltpu.make_async_remote_copy(
            src_ref=source,
            dst_ref=target,
            send_sem=send_sems.at[phase, k, j],
            recv_sem=recv_sems.at[phase, k, j],
            device_id={"blk": lax.rem(me + j, owners)},
            device_id_type=MESH,
        )

    def wait_arrivals(phase, k, target):
        for j in range(1, owners):
            block_copy(phase, k, j, target, target).wait_recv()

    def ask_copy(j):
        return pltpu.make_async_remote_copy(
            src_ref=wanted_ref,
            dst_ref=asked_vmem.at[me],
            send_sem=ask_send.at[j],
            recv_sem=ask_recv.at[j],
            device_id={"blk": lax.rem(me + j, owners)},
            device_id_type=MESH,
        )

    for j in range(1, owners):
        ask_copy(j).start()
    asked_vmem[me] = wanted_ref[...]
    for j in range(1, owners):
        ask_copy(j).wait_recv()
    move = pltpu.make_async_copy(asked_vmem, asked_smem, load_sems.at[4])
    move.start()
    move.wait()
    loads[0].wait()

    def asked(r):
        return asked_smem[r, 0, me]

    def send_panels(k, _):
        def gather(r, _):
            slots_before[k, r] = pool[asked(r), :, columns(k)]
            return 0

        lax.fori_loop(0, owners, gather, 0)
        for j in range(1, owners):
            block_copy(
                0, k, j, slots_before.at[k, lax.rem(me + j, owners)], panels.at[0, k, me]
            ).start()
        panels[0, k, me] = slots_before[k, me]
        return 0

    lax.fori_loop(0, chunks, send_panels, 0)

    def choose(b, _):
        place = b
        for r in range(owners):
            place = jnp.where(asked(r) == b, owned_blocks + r, place)
        chosen[b] = place
        return 0

    lax.fori_loop(0, owned_blocks, choose, 0)
    for load in loads[1:]:
        load.wait()

    half = lax.broadcasted_iota(jnp.int32, (pattern_rows, lanes), 1) // block_width

    def matches(s, m):
        return support_ref[:, s:s + 1] == half + m * per_lane

    def spread(codes_now):
        pieces = []
        for s in range(support_count):
            piece = codes_now[:, s * block_width:(s + 1) * block_width]
            pieces.append(jnp.concatenate([piece] * per_lane, axis=1))
        for m in range(owners // per_lane):
            total = jnp.zeros((pattern_rows, lanes), jnp.float32)
            for s in range(support_count):
                total = jnp.where(matches(s, m), pieces[s], total)
            dense[:, m * lanes:(m + 1) * lanes] = total.astype(jnp.bfloat16)

    def pick():
        pieces = []
        for s in range(support_count):
            total = jnp.zeros((pattern_rows, lanes), jnp.float32)
            for m in range(owners // per_lane):
                total = jnp.where(matches(s, m), correlated[:, m * lanes:(m + 1) * lanes], total)
            folded = total[:, :block_width]
            for h in range(1, per_lane):
                folded = folded + total[:, h * block_width:(h + 1) * block_width]
            pieces.append(folded)
        return scale_factor * jnp.concatenate(pieces, axis=1)

    def code_copy(step, j):
        return pltpu.make_async_remote_copy(
            src_ref=code_parts.at[step, my_row],
            dst_ref=code_parts.at[step, my_row],
            send_sem=code_send.at[step, j],
            recv_sem=code_recv.at[step, j],
            device_id={"rows": lax.rem(my_row + j, row_count)},
            device_id_type=MESH,
        )

    codes_out[...] = codes_ref[...].astype(jnp.float32)

    for step in range(2):
        spread(codes_out[...].astype(jnp.bfloat16).astype(jnp.float32))
        correlated[...] = jnp.zeros_like(correlated)

        def region_chunk(k, _, step=step):
            wait_arrivals(2 * step, k, panels.at[step, k, 0])
            panel = panels[step, k].reshape(owners * block_width, chunk)
            coefficients = dense[...]
            rebuilt = scale_factor * jnp.dot(
                coefficients, panel, preferred_element_type=jnp.float32
            )
            residual = (patterns_ref[:, columns(k)].astype(jnp.float32) - rebuilt).astype(
                jnp.bfloat16
            )
            atom_terms = scale_factor * lax.dot_general(
                coefficients, residual, (((0,), (0,)), ((), ())),
                preferred_element_type=jnp.float32,
            )
            terms[step, k] = atom_terms.astype(jnp.bfloat16).reshape(owners, block_width, chunk)
            for j in range(1, owners):
                block_copy(
                    2 * step + 1, k, j,
                    terms.at[step, k, lax.rem(me + j, owners)],
                    arrived.at[step, k, me],
                ).start()
            arrived[step, k, me] = terms[step, k, me]
            correlated[...] += lax.dot_general(
                residual, panel, (((1,), (1,)), ((), ())), preferred_element_type=jnp.float32
            )
            return 0

        lax.fori_loop(0, chunks, region_chunk, 0)
        code_parts[step, my_row] = pick().astype(jnp.bfloat16)
        for j in range(1, row_count):
            code_copy(step, j).start()

        def owner_chunk(k, _, step=step):
            wait_arrivals(2 * step + 1, k, arrived.at[step, k, 0])

            def one_slot(r, _):
                total = jnp.zeros((block_width, chunk), jnp.float32)
                for q in range(owners):
                    same = jnp.where(asked(r) == asked(q), 1.0, 0.0).astype(jnp.float32)
                    total = total + same * arrived[step, k, q].astype(jnp.float32)
                before = slots_before[k, r] if step == 0 else slots_next[k, r]
                after = (before.astype(jnp.float32) + ATOM_RATE * total).astype(jnp.bfloat16)
                if step == 0:
                    slots_next[k, r] = after
                else:
                    pool[owned_blocks + r, :, columns(k)] = after
                return 0

            lax.fori_loop(0, owners, one_slot, 0)
            if step == 0:
                for j in range(1, owners):
                    block_copy(
                        2, k, j,
                        slots_next.at[k, lax.rem(me + j, owners)],
                        panels.at[1, k, me],
                    ).start()
                panels[1, k, me] = slots_next[k, me]
            return 0

        lax.fori_loop(0, chunks, owner_chunk, 0)
        for j in range(1, row_count):
            code_copy(step, j).wait_recv()
        total = code_parts[step, 0].astype(jnp.float32)
        for i in range(1, row_count):
            total = total + code_parts[step, i].astype(jnp.float32)
        codes_out[...] += CODE_RATE * total

    def place_block(b, _):
        dictionary_out[b] = pool[chosen[b]]
        return 0

    lax.fori_loop(0, owned_blocks, place_block, 0)

    def drain(k, _):
        for phase in range(4):
            for j in range(1, owners):
                block_copy(phase, k, j, terms.at[0, k, 0], terms.at[0, k, 0]).wait_send()
        return 0

    lax.fori_loop(0, chunks, drain, 0)
    for step in range(2):
        for j in range(1, row_count):
            code_copy(step, j).wait_send()
    for j in range(1, owners):
        ask_copy(j).wait_send()


def local(patterns, dictionary, codes, support, wanted):
    owners = lax.axis_size("blk")
    row_count = lax.axis_size("rows")
    pattern_rows, pixel_count = patterns.shape
    support_count = support.shape[1]
    code_width = codes.shape[1]
    block_width = code_width // support_count
    owned_blocks = dictionary.shape[0] // block_width
    scale_factor = code_width ** (-0.5)
    chunk = min(CHUNK, pixel_count)
    chunks = pixel_count // chunk
    blocks = dictionary.reshape(owned_blocks, block_width, pixel_count)
    vmem = pl.BlockSpec(memory_space=pltpu.VMEM)
    bf16 = jnp.bfloat16
    hbm = pl.BlockSpec(memory_space=pl.ANY)
    dictionary_after, codes_after = pl.pallas_call(
        functools.partial(steps_kernel, owners, row_count, block_width, chunk, scale_factor),
        out_shape=(
            jax.ShapeDtypeStruct((owned_blocks, block_width, pixel_count), bf16),
            jax.ShapeDtypeStruct((pattern_rows, code_width), jnp.float32),
        ),
        in_specs=[vmem] + [hbm] * 4,
        out_specs=(vmem, vmem),
        scratch_shapes=[
            pltpu.VMEM(support.shape, jnp.int32),
            pltpu.VMEM(codes.shape, bf16),
            pltpu.VMEM(patterns.shape, bf16),
            pltpu.VMEM((owned_blocks + owners, block_width, pixel_count), bf16),
            pltpu.VMEM((owners,) + wanted.shape, jnp.int32),
            pltpu.SMEM((owners,) + wanted.shape, jnp.int32),
            pltpu.SMEM((owned_blocks,), jnp.int32),
            pltpu.VMEM((2, chunks, owners, block_width, chunk), bf16),
            pltpu.VMEM((2, chunks, owners, block_width, chunk), bf16),
            pltpu.VMEM((2, chunks, owners, block_width, chunk), bf16),
            pltpu.VMEM((chunks, owners, block_width, chunk), bf16),
            pltpu.VMEM((chunks, owners, block_width, chunk), bf16),
            pltpu.VMEM((pattern_rows, owners * block_width), bf16),
            pltpu.VMEM((pattern_rows, owners * block_width), jnp.float32),
            pltpu.VMEM((2, row_count, pattern_rows, code_width), bf16),
            pltpu.SemaphoreType.DMA((4, chunks, owners)),
            pltpu.SemaphoreType.DMA((4, chunks, owners)),
            pltpu.SemaphoreType.DMA((2, row_count)),
            pltpu.SemaphoreType.DMA((2, row_count)),
            pltpu.SemaphoreType.DMA((owners,)),
            pltpu.SemaphoreType.DMA((owners,)),
            pltpu.SemaphoreType.DMA((5,)),
        ],
        compiler_params=pltpu.CompilerParams(
            collective_id=0, has_side_effects=True, vmem_limit_bytes=60 * 1024 * 1024
        ),
    )(wanted, support, codes, patterns, blocks)
    return (dictionary_after.reshape(dictionary.shape), codes_after)


def solution(mesh):
    placed = (P("blk", "rows"), P("blk", "rows"), P("blk", None), P("blk", None), P("blk", None))
    return jax.shard_map(
        local,
        mesh=mesh,
        in_specs=placed,
        out_specs=(P("blk", "rows"), P("blk", None)),
        check_vma=False,
    )
```

```python
import functools

import jax
import jax.numpy as jnp
from jax import lax
from jax.experimental import pallas as pl
from jax.experimental.pallas import tpu as pltpu
from jax.sharding import PartitionSpec as P

CODE_RATE = 0.05
ATOM_RATE = 0.2
CHUNK = 256
MESH = pl.DeviceIdType.MESH


def steps_kernel(
    owners, row_count, block_width, chunk, scale_factor,
    wanted_ref, support_hbm, codes_hbm, patterns_hbm, dictionary_hbm,
    dictionary_out, codes_out,
    support_ref, codes_ref, patterns_ref, pool, asked_vmem, asked_smem, chosen,
    panels, arrived, terms, slots_before, slots_next, dense, correlated, code_parts,
    send_sems, recv_sems, code_send, code_recv, ask_send, ask_recv, load_sems,
):
    me = lax.axis_index("blk")
    my_row = lax.axis_index("rows")
    pattern_rows, pixel_count = patterns_ref.shape
    owned_blocks = dictionary_out.shape[0]
    chunks = pixel_count // chunk
    loads = (
        pltpu.make_async_copy(
            dictionary_hbm, pool.at[pl.ds(0, owned_blocks)], load_sems.at[0]
        ),
        pltpu.make_async_copy(codes_hbm, codes_ref, load_sems.at[1]),
        pltpu.make_async_copy(support_hbm, support_ref, load_sems.at[2]),
        pltpu.make_async_copy(patterns_hbm, patterns_ref, load_sems.at[3]),
    )
    for load in loads:
        load.start()
    support_count = support_ref.shape[0]
    lanes = 128
    per_lane = lanes // block_width

    barrier = pltpu.get_barrier_semaphore()
    for j in range(1, owners):
        pl.semaphore_signal(
            barrier, inc=1, device_id={"blk": lax.rem(me + j, owners)}, device_id_type=MESH
        )
    for j in range(1, row_count):
        pl.semaphore_signal(
            barrier, inc=1, device_id={"rows": lax.rem(my_row + j, row_count)}, device_id_type=MESH
        )
    pl.semaphore_wait(barrier, owners + row_count - 2)

    def columns(k):
        return pl.ds(pl.multiple_of(k * chunk, chunk), chunk)

    def block_copy(phase, k, j, source, target):
        return pltpu.make_async_remote_copy(
            src_ref=source,
            dst_ref=target,
            send_sem=send_sems.at[phase, k, j],
            recv_sem=recv_sems.at[phase, k, j],
            device_id={"blk": lax.rem(me + j, owners)},
            device_id_type=MESH,
        )

    def wait_arrivals(phase, k, target):
        for j in range(1, owners):
            block_copy(phase, k, j, target, target).wait_recv()

    def ask_copy(j):
        return pltpu.make_async_remote_copy(
            src_ref=wanted_ref,
            dst_ref=asked_vmem.at[me],
            send_sem=ask_send.at[j],
            recv_sem=ask_recv.at[j],
            device_id={"blk": lax.rem(me + j, owners)},
            device_id_type=MESH,
        )

    for j in range(1, owners):
        ask_copy(j).start()
    asked_vmem[me] = wanted_ref[...]
    for j in range(1, owners):
        ask_copy(j).wait_recv()
    move = pltpu.make_async_copy(asked_vmem, asked_smem, load_sems.at[4])
    move.start()
    move.wait()
    loads[0].wait()

    def asked(r):
        return asked_smem[r, 0, me]

    def send_panels(k, _):
        def gather(r, _):
            slots_before[k, r] = pool[asked(r), :, columns(k)]
            return 0

        lax.fori_loop(0, owners, gather, 0)
        for j in range(1, owners):
            block_copy(
                0, k, j, slots_before.at[k, lax.rem(me + j, owners)], panels.at[0, k, me]
            ).start()
        panels[0, k, me] = slots_before[k, me]
        return 0

    lax.fori_loop(0, chunks, send_panels, 0)

    def choose(b, _):
        place = b
        for r in range(owners):
            place = jnp.where(asked(r) == b, owned_blocks + r, place)
        chosen[b] = place
        return 0

    lax.fori_loop(0, owned_blocks, choose, 0)

    for load in loads[1:]:
        load.wait()
    support_now = support_ref[...].T
    half = lax.broadcasted_iota(jnp.int32, (pattern_rows, lanes), 1) // block_width

    def matches(s, m):
        return support_now[:, s:s + 1] == half + m * per_lane

    def spread(codes_now):
        pieces = []
        for s in range(support_count):
            piece = codes_now[:, s * block_width:(s + 1) * block_width]
            pieces.append(jnp.concatenate([piece] * per_lane, axis=1))
        for m in range(owners // per_lane):
            total = jnp.zeros((pattern_rows, lanes), jnp.float32)
            for s in range(support_count):
                total = jnp.where(matches(s, m), pieces[s], total)
            dense[:, m * lanes:(m + 1) * lanes] = total.astype(jnp.bfloat16)

    def pick():
        pieces = []
        for s in range(support_count):
            total = jnp.zeros((pattern_rows, lanes), jnp.float32)
            for m in range(owners // per_lane):
                total = jnp.where(matches(s, m), correlated[:, m * lanes:(m + 1) * lanes], total)
            folded = total[:, :block_width]
            for h in range(1, per_lane):
                folded = folded + total[:, h * block_width:(h + 1) * block_width]
            pieces.append(folded)
        return scale_factor * jnp.concatenate(pieces, axis=1)

    def code_copy(step, j):
        return pltpu.make_async_remote_copy(
            src_ref=code_parts.at[step, my_row],
            dst_ref=code_parts.at[step, my_row],
            send_sem=code_send.at[step, j],
            recv_sem=code_recv.at[step, j],
            device_id={"rows": lax.rem(my_row + j, row_count)},
            device_id_type=MESH,
        )

    codes_out[...] = codes_ref[...].astype(jnp.float32)

    for step in range(2):
        spread(codes_out[...].astype(jnp.bfloat16).astype(jnp.float32))
        correlated[...] = jnp.zeros_like(correlated)

        def region_chunk(k, _, step=step):
            wait_arrivals(2 * step, k, panels.at[step, k, 0])
            panel = panels[step, k].reshape(owners * block_width, chunk)
            coefficients = dense[...]
            rebuilt = scale_factor * jnp.dot(
                coefficients, panel, preferred_element_type=jnp.float32
            )
            residual = (patterns_ref[:, columns(k)].astype(jnp.float32) - rebuilt).astype(
                jnp.bfloat16
            )
            atom_terms = scale_factor * lax.dot_general(
                coefficients, residual, (((0,), (0,)), ((), ())),
                preferred_element_type=jnp.float32,
            )
            terms[step, k] = atom_terms.astype(jnp.bfloat16).reshape(owners, block_width, chunk)
            for j in range(1, owners):
                block_copy(
                    2 * step + 1, k, j,
                    terms.at[step, k, lax.rem(me + j, owners)],
                    arrived.at[step, k, me],
                ).start()
            arrived[step, k, me] = terms[step, k, me]
            correlated[...] += lax.dot_general(
                residual, panel, (((1,), (1,)), ((), ())), preferred_element_type=jnp.float32
            )
            return 0

        lax.fori_loop(0, chunks, region_chunk, 0)
        code_parts[step, my_row] = pick().astype(jnp.bfloat16)
        for j in range(1, row_count):
            code_copy(step, j).start()

        def owner_chunk(k, _, step=step):
            wait_arrivals(2 * step + 1, k, arrived.at[step, k, 0])

            def one_slot(r, _):
                total = jnp.zeros((block_width, chunk), jnp.float32)
                for q in range(owners):
                    same = jnp.where(asked(r) == asked(q), 1.0, 0.0).astype(jnp.float32)
                    total = total + same * arrived[step, k, q].astype(jnp.float32)
                before = slots_before[k, r] if step == 0 else slots_next[k, r]
                after = (before.astype(jnp.float32) + ATOM_RATE * total).astype(jnp.bfloat16)
                if step == 0:
                    slots_next[k, r] = after
                else:
                    pool[owned_blocks + r, :, columns(k)] = after
                return 0

            lax.fori_loop(0, owners, one_slot, 0)
            if step == 0:
                for j in range(1, owners):
                    block_copy(
                        2, k, j,
                        slots_next.at[k, lax.rem(me + j, owners)],
                        panels.at[1, k, me],
                    ).start()
                panels[1, k, me] = slots_next[k, me]
            return 0

        lax.fori_loop(0, chunks, owner_chunk, 0)
        for j in range(1, row_count):
            code_copy(step, j).wait_recv()
        total = code_parts[step, 0].astype(jnp.float32)
        for i in range(1, row_count):
            total = total + code_parts[step, i].astype(jnp.float32)
        codes_out[...] += CODE_RATE * total

    def place_block(b, _):
        dictionary_out[b] = pool[chosen[b]]
        return 0

    lax.fori_loop(0, owned_blocks, place_block, 0)

    def drain(k, _):
        for phase in range(4):
            for j in range(1, owners):
                block_copy(phase, k, j, terms.at[0, k, 0], terms.at[0, k, 0]).wait_send()
        return 0

    lax.fori_loop(0, chunks, drain, 0)
    for step in range(2):
        for j in range(1, row_count):
            code_copy(step, j).wait_send()
    for j in range(1, owners):
        ask_copy(j).wait_send()


def local(patterns, dictionary, codes, support, wanted):
    owners = lax.axis_size("blk")
    row_count = lax.axis_size("rows")
    pattern_rows, pixel_count = patterns.shape
    support_count = support.shape[1]
    code_width = codes.shape[1]
    block_width = code_width // support_count
    owned_blocks = dictionary.shape[0] // block_width
    scale_factor = code_width ** (-0.5)
    chunk = min(CHUNK, pixel_count)
    chunks = pixel_count // chunk
    blocks = dictionary.reshape(owned_blocks, block_width, pixel_count)
    vmem = pl.BlockSpec(memory_space=pltpu.VMEM)
    bf16 = jnp.bfloat16
    hbm = pl.BlockSpec(memory_space=pltpu.HBM)
    dictionary_after, codes_after = pl.pallas_call(
        functools.partial(steps_kernel, owners, row_count, block_width, chunk, scale_factor),
        out_shape=(
            jax.ShapeDtypeStruct((owned_blocks, block_width, pixel_count), bf16),
            jax.ShapeDtypeStruct((pattern_rows, code_width), jnp.float32),
        ),
        in_specs=[vmem] + [hbm] * 4,
        out_specs=(vmem, vmem),
        scratch_shapes=[
            pltpu.VMEM(support.shape[::-1], jnp.int32),
            pltpu.VMEM(codes.shape, bf16),
            pltpu.VMEM(patterns.shape, bf16),
            pltpu.VMEM((owned_blocks + owners, block_width, pixel_count), bf16),
            pltpu.VMEM((owners,) + wanted.shape, jnp.int32),
            pltpu.SMEM((owners,) + wanted.shape, jnp.int32),
            pltpu.SMEM((owned_blocks,), jnp.int32),
            pltpu.VMEM((2, chunks, owners, block_width, chunk), bf16),
            pltpu.VMEM((2, chunks, owners, block_width, chunk), bf16),
            pltpu.VMEM((2, chunks, owners, block_width, chunk), bf16),
            pltpu.VMEM((chunks, owners, block_width, chunk), bf16),
            pltpu.VMEM((chunks, owners, block_width, chunk), bf16),
            pltpu.VMEM((pattern_rows, owners * block_width), bf16),
            pltpu.VMEM((pattern_rows, owners * block_width), jnp.float32),
            pltpu.VMEM((2, row_count, pattern_rows, code_width), bf16),
            pltpu.SemaphoreType.DMA((4, chunks, owners)),
            pltpu.SemaphoreType.DMA((4, chunks, owners)),
            pltpu.SemaphoreType.DMA((2, row_count)),
            pltpu.SemaphoreType.DMA((2, row_count)),
            pltpu.SemaphoreType.DMA((owners,)),
            pltpu.SemaphoreType.DMA((owners,)),
            pltpu.SemaphoreType.DMA((5,)),
        ],
        compiler_params=pltpu.CompilerParams(
            collective_id=0, has_side_effects=True, vmem_limit_bytes=47 * 1024 * 1024
        ),
    )(wanted, support.T, codes, patterns, blocks)
    return (dictionary_after.reshape(dictionary.shape), codes_after)


def solution(mesh):
    placed = (P("blk", "rows"), P("blk", "rows"), P("blk", None), P("blk", None), P("blk", None))
    return jax.shard_map(
        local,
        mesh=mesh,
        in_specs=placed,
        out_specs=(P("blk", "rows"), P("blk", None)),
        check_vma=False,
    )
```
